256 devices in a mesh: row: 32 (over y, z), col: 8 (over x, core).
Axes of the slice: x: 4, y: 4, z: 8, core: 2. Of those that a mesh axis runs over, the one named last changes fastest.
Arguments:
- load_currents: float32 [16, 256, 128, 128], P(None, 'row', 'col'), may hold values from -24 to 24
- block_library: float32 [8, 128, 128], replicated, may hold values from -4.0625 to 24.1, as said below
- strap_conductance: float32 [2, 128], replicated, may hold values from 0.5 to 4
- block_types: int32 [256, 128], P('row', 'col'), may hold values from 0 to 7
- aggregate_map: int32 [256, 128], P('row', 'col'), may hold values from 0 to 255, as said below
Outputs:
- node_voltage: float32 [16, 256, 128, 128], P(None, 'row', 'col')
- residual: float32 [16, 256, 128, 128], P(None, 'row', 'col')
The draws below stay inside these ranges and needn't reach their ends.
Inputs may be any that keep to these rules, and one draw needn't show every extreme that they name: `aggregate_map`: each aggregate id names an aggregate of one column group of 16 block columns; the same id in another column group is another aggregate. Every aggregate of every column group holds at least one block. `block_library`: each library block is symmetric positive definite, with nonpositive off-diagonal entries and positive row sums.
All inputs are finite; a program needn't handle non-finite values.
Results may differ from the reference program's by a relative error of at most 0.0003.
Values sent between devices are 32-bit elements; how exact they have to be, the bound alone decides.
A program may use at most 64 MiB of HBM per device.

```python
import math
import jax
import jax.numpy as jnp
from jax import lax

NODE = 128
LAYERS = 8
SIZ = 16
BC = 16
NT = 8
SWEEPS = 3
ITERS = 2
AGR = 4
AGC = 4
GR = 256
GC = 128
NAGG = 256
N_COL = 8


def draw_load_currents(key, part):
    first, second, third = jax.random.split(key, 3)
    grow = jnp.arange(GR, dtype=jnp.float32)[:, None]
    ramp = 1.0 + 2.0 * grow / max(GR - 1, 1)
    block_scale = 10.0 ** (jax.random.uniform(second, (GR, GC), dtype=jnp.float32) - 1.0) * ramp
    sizing_scale = jax.random.uniform(third, (SIZ, 1, 1, 1), dtype=jnp.float32, minval=0.5, maxval=2.0)
    rough = jnp.clip(jax.random.normal(first, (SIZ, GR, GC, NODE), dtype=jnp.float32), -4.0, 4.0)
    return (rough * block_scale[None, :, :, None] * sizing_scale).astype(jnp.float32)


def log_uniform(key, shape, low, high):
    exponent = jax.random.uniform(key, shape, dtype=jnp.float32, minval=math.log(low), maxval=math.log(high))
    return jnp.exp(exponent)


def draw_block_library(key, part):
    key_lateral, key_via, key_pad, key_leak, key_distant = jax.random.split(key, 5)
    per_layer = NODE // LAYERS
    lateral_wire = log_uniform(key_lateral, (NT, LAYERS, per_layer), 0.5, 4.0)
    via_wire = log_uniform(key_via, (NT, LAYERS, per_layer), 0.5, 4.0)
    pad_ground = log_uniform(key_pad, (NT, 1, per_layer), 0.5, 2.0)
    leakage = log_uniform(key_leak, (NT, NODE), 0.02, 0.1)
    position = jnp.arange(per_layer, dtype=jnp.int32)[None, None, :]
    layer_index = jnp.arange(LAYERS, dtype=jnp.int32)[None, :, None]
    lateral_wire = jnp.where(position < per_layer - 1, lateral_wire, 0.0)
    via_wire = jnp.where(layer_index < LAYERS - 1, via_wire, 0.0)
    lateral_before = jnp.concatenate([jnp.zeros((NT, LAYERS, 1), jnp.float32), lateral_wire[:, :, :-1]], axis=2)
    via_before = jnp.concatenate([jnp.zeros((NT, 1, per_layer), jnp.float32), via_wire[:, :-1, :]], axis=1)
    degree = (lateral_wire + lateral_before + via_wire + via_before).reshape(NT, NODE)
    ground = leakage + jnp.concatenate([pad_ground, jnp.zeros((NT, LAYERS - 1, per_layer), jnp.float32)], axis=1).reshape(NT, NODE)
    lateral_flat = lateral_wire.reshape(NT, NODE)
    via_flat = via_wire.reshape(NT, NODE)
    row_index = jnp.arange(NODE, dtype=jnp.int32)[:, None]
    col_index = jnp.arange(NODE, dtype=jnp.int32)[None, :]
    right_next = (col_index == row_index + 1).astype(jnp.float32)
    left_next = (row_index == col_index + 1).astype(jnp.float32)
    layer_below = (col_index == row_index + per_layer).astype(jnp.float32)
    layer_above = (row_index == col_index + per_layer).astype(jnp.float32)
    sparse_part = lateral_flat[:, :, None] * right_next + lateral_flat[:, None, :] * left_next + via_flat[:, :, None] * layer_below + via_flat[:, None, :] * layer_above
    integer_counts = jax.random.randint(key_distant, (NT, NODE, NODE), 0, 65)
    paired = integer_counts + jnp.swapaxes(integer_counts, 1, 2)
    paired = jnp.where(row_index == col_index, 0, paired)
    far_unit = 1.0 / 2048.0
    distant = paired.astype(jnp.float32) * far_unit
    distant_total = jnp.sum(paired, axis=2).astype(jnp.float32) * far_unit
    identity = (row_index == col_index).astype(jnp.float32)
    centre = degree + distant_total + ground
    return (identity * centre[:, :, None] - sparse_part - distant).astype(jnp.float32)


def draw_aggregate_map(key, part):
    first, second = jax.random.split(key, 2)
    grow = jnp.arange(GR, dtype=jnp.int32)[:, None]
    gcol = jnp.arange(GC, dtype=jnp.int32)[None, :]
    leading = (grow % AGR != 0).astype(jnp.int32)
    jitter = jax.random.randint(first, (GR, GC), 0, 2) * leading
    bands = GR // AGR
    half_span = bands // 2
    band = (grow // AGR + jitter * half_span) % bands
    region = band * (BC // AGC) + gcol % BC // AGC
    labels = jax.random.permutation(second, NAGG)
    return labels[region].astype(jnp.int32)


def touch_ends(values, own_key, least, top_value):
    longest = values.shape.index(max(values.shape))
    spots = []
    for shift in (0, 1):
        where = [jax.random.randint(jax.random.fold_in(own_key, axis), (), 0, length) for axis, length in enumerate(values.shape)]
        where[longest] = (where[longest] + shift) % values.shape[longest]
        spots.append(tuple(where))
    return values.at[spots[0]].set(least).at[spots[1]].set(top_value)


def setup_inputs(seed: int = 0) -> dict:
    arg_keys = jax.random.split(jax.random.key(seed), 6)
    return {
        "load_currents": draw_load_currents(jax.random.fold_in(arg_keys[5], 71), 0),
        "block_library": draw_block_library(jax.random.fold_in(arg_keys[5], 71), 0),
        "strap_conductance": jnp.clip(jnp.exp(jax.random.uniform(arg_keys[2], (2, NODE), jnp.float32, math.log(0.5), math.log(4.0))), 0.5, 4.0),
        "block_types": touch_ends(jax.random.randint(arg_keys[3], (GR, GC), 0, NT), jax.random.fold_in(arg_keys[3], 1), 0, NT - 1).astype(jnp.int32),
        "aggregate_map": draw_aggregate_map(jax.random.fold_in(arg_keys[5], 71), 0),
    }


def block_products(block_library, block_types, field):

    def one_row(pair):
        row_field, row_types = pair
        picked = block_library[row_types]
        return jnp.einsum('cij,scj->sci', picked, row_field, precision=lax.Precision.HIGHEST)
    rows = lax.map(one_row, (jnp.moveaxis(field, 1, 0), block_types))
    return jnp.moveaxis(rows, 0, 1)

def operator(block_library, block_types, strap_conductance, field):
    padded = jnp.pad(field, ((0, 0), (1, 1), (1, 1), (0, 0)))
    north = padded[:, :-2, 1:-1]
    south = padded[:, 2:, 1:-1]
    west = padded[:, 1:-1, :-2]
    east = padded[:, 1:-1, 2:]
    lateral = strap_conductance[0] * (2.0 * field - north - south) + strap_conductance[1] * (2.0 * field - west - east)
    return block_products(block_library, block_types, field) + lateral

def coarse_terms(group_ids, group_types, block_sums, north_weight, east_weight, count):
    centre = block_sums[group_types] + 2.0 * north_weight + 2.0 * east_weight
    flat = group_ids.reshape(-1)
    upper = group_ids[:-1].reshape(-1)
    lower = group_ids[1:].reshape(-1)
    left = group_ids[:, :-1].reshape(-1)
    right = group_ids[:, 1:].reshape(-1)
    index = jnp.concatenate([flat * count + flat, upper * count + lower, lower * count + upper, left * count + right, right * count + left]).astype(jnp.int32)
    values = jnp.concatenate([centre.reshape(-1), -north_weight * jnp.ones((2 * upper.shape[0],), jnp.float32), -east_weight * jnp.ones((2 * left.shape[0],), jnp.float32)])
    return jax.ops.segment_sum(values, index, num_segments=count * count).reshape(count, count)

def reference(load_currents, block_library, strap_conductance, block_types, aggregate_map):
    couple = 2.0 * strap_conductance[0] + 2.0 * strap_conductance[1]
    diag_library = jnp.diagonal(block_library, axis1=1, axis2=2)
    diagonal = diag_library[block_types] + couple
    block_sums = jnp.sum(block_library, axis=(1, 2))
    north_weight = jnp.sum(strap_conductance[0])
    east_weight = jnp.sum(strap_conductance[1])
    factors = []
    for group in range(N_COL):
        group_ids = aggregate_map[:, group * BC:(group + 1) * BC]
        group_types = block_types[:, group * BC:(group + 1) * BC]
        matrix = coarse_terms(group_ids, group_types, block_sums, north_weight, east_weight, NAGG)
        factors.append(jnp.linalg.cholesky(matrix))

    def smooth(residual):
        result = residual / diagonal
        for sweep in range(SWEEPS - 1):
            image = block_products(block_library, block_types, result) + couple * result
            result = result + (residual - image) / diagonal
        return result

    def coarse_part(residual):
        sums = residual.sum(-1)
        pieces = []
        for group in range(N_COL):
            group_ids = aggregate_map[:, group * BC:(group + 1) * BC].reshape(-1)
            local = sums[:, :, group * BC:(group + 1) * BC].reshape(SIZ, -1).T
            gathered = jax.ops.segment_sum(local, group_ids, num_segments=NAGG)
            solved = jax.scipy.linalg.cho_solve((factors[group], True), gathered)
            pieces.append(solved[group_ids].T.reshape(SIZ, GR, BC))
        return jnp.concatenate(pieces, axis=2)[..., None]

    def precondition(residual):
        return smooth(residual) + coarse_part(residual)
    node_voltage = jnp.zeros_like(load_currents)
    residual = load_currents
    zeta = precondition(residual)
    direction = zeta
    aligned = jnp.sum(residual * zeta, axis=(1, 2, 3))
    for iteration in range(ITERS):
        image = operator(block_library, block_types, strap_conductance, direction)
        curvature = jnp.sum(direction * image, axis=(1, 2, 3))
        step_size = (aligned / curvature)[:, None, None, None]
        node_voltage = node_voltage + step_size * direction
        residual = residual - step_size * image
        if iteration + 1 < ITERS:
            zeta = precondition(residual)
            fresh = jnp.sum(residual * zeta, axis=(1, 2, 3))
            blend = (fresh / aligned)[:, None, None, None]
            direction = zeta + blend * direction
            aligned = fresh
    return (node_voltage, residual)
```

```python
import functools
import jax
import jax.numpy as jnp
from jax import lax
from jax.experimental import pallas as pl
from jax.experimental.pallas import tpu as pltpu
from jax.sharding import PartitionSpec as P

MESH = pl.DeviceIdType.MESH
F32 = jnp.float32
BF = jnp.bfloat16
LAST = (((1,), (1,)), ((), ()))
PLAIN = (((1,), (0,)), ((), ()))
NEWTON = 6
REFINE = 2
AGR = 4
AGC = 4


def iota(shape, dim):
    return lax.broadcasted_iota(jnp.int32, shape, dim)


def onehot(mask):
    return jnp.where(mask, 1.0, 0.0).astype(BF)


def split2(x):
    hi = x.astype(BF)
    lo = (x - hi.astype(F32)).astype(BF)
    return hi, lo


def split3(x):
    hi = x.astype(BF)
    rest = x - hi.astype(F32)
    mid = rest.astype(BF)
    lo = (rest - mid.astype(F32)).astype(BF)
    return hi, mid, lo


def dot(a, b, dims=PLAIN):
    return lax.dot_general(a, b, dims, preferred_element_type=F32)


def rows_dot(x, table, dims):
    m = x.shape[0]
    y = dot(jnp.concatenate(split3(x), axis=0), table, dims)
    return y[:m] + y[m : 2 * m] + y[2 * m :]


def cols_dot(table, x):
    m = x.shape[0]
    y = dot(table, jnp.concatenate(split3(x), axis=0), LAST)
    return y[:, :m] + y[:, m : 2 * m] + y[:, 2 * m :]


def kernel(
    n_r, n_c,
    r_ref, lib_ref, strap_ref, typ_ref, ids_ref,
    v_ref, res_ref,
    z_ref, u_ref, w_ref, t_ref,
    lib_w, inv_t, cop_t, typ_t, rs_t,
    own_idt, gat_idt, own_rho, gat_rho, own_tau, gat_tau,
    idsh, oh_all, acc, dacc, mat, mat_h, xmat,
    edge_out, halo_ns, halo_ew,
    cedge_out, cedge_in,
    dots, own_sum, row_sum, own_col, col_sum,
    send_idt, recv_idt, send_rho, recv_rho, send_tau, recv_tau,
    send_halo, recv_halo, send_edge, recv_edge,
    send_rs, recv_rs, send_cs, recv_cs,
):
    sz, rl, cl, nd = r_ref.shape
    nb = rl * cl
    nt = lib_ref.shape[0]
    ng = acc.shape[0]
    me = lax.axis_index("row")
    mc = lax.axis_index("col")

    def row_peer(off):
        return {"row": lax.rem(me + off, n_r)}

    def col_peer(off):
        return {"col": lax.rem(mc + off, n_c)}

    barrier = pltpu.get_barrier_semaphore()

    def greet_row(off, carry):
        pl.semaphore_signal(barrier, inc=1, device_id=row_peer(off), device_id_type=MESH)
        return carry

    def greet_col(off, carry):
        pl.semaphore_signal(barrier, inc=1, device_id=col_peer(off), device_id_type=MESH)
        return carry

    lax.fori_loop(1, n_r, greet_row, 0)
    lax.fori_loop(1, n_c, greet_col, 0)

    strap0 = strap_ref[0:1, :]
    strap1 = strap_ref[1:2, :]
    couple = 2.0 * strap0 + 2.0 * strap1
    nw = jnp.sum(strap0, axis=1, keepdims=True)
    ew = jnp.sum(strap1, axis=1, keepdims=True)
    eye = iota((nd, nd), 0) == iota((nd, nd), 1)
    spread = onehot(iota((cl, nb), 0) == lax.rem(iota((cl, nb), 1), cl))
    mine = iota((rl, nb), 0) == iota((rl, nb), 1) // cl

    def flat_row(ref):
        wide = dot(ref[...].astype(F32).astype(BF), spread)
        return jnp.sum(jnp.where(mine, wide, 0.0), axis=0, keepdims=True)

    id_row = flat_row(ids_ref)
    typ_row = flat_row(typ_ref)
    own_idt[0:1, :] = id_row
    own_idt[1:2, :] = typ_row

    def column(row):
        return jnp.transpose(jnp.broadcast_to(row, (nb, nb)))

    typ = column(typ_row)
    typ_t[...] = typ
    diag = jnp.zeros((nb, nd), F32)
    rsum = jnp.zeros((nb, nd), F32)
    sums = []
    for t in range(nt):
        lib = lib_ref[t]
        hi, lo = split2(lib)
        half = (t % 2) * nd
        lib_w[t // 2, 0:nd, half : half + nd] = hi
        lib_w[t // 2, nd : 2 * nd, half : half + nd] = hi
        lib_w[t // 2, 2 * nd : 3 * nd, half : half + nd] = lo
        rows = jnp.sum(lib, axis=0, keepdims=True)
        sums.append(jnp.sum(rows, axis=1, keepdims=True))
        diag = jnp.where(typ == t, jnp.sum(jnp.where(eye, lib, 0.0), axis=0, keepdims=True), diag)
        rsum = jnp.where(typ == t, rows, rsum)
    inv_t[...] = 1.0 / (diag + couple)
    cop_t[...] = jnp.broadcast_to(couple, (nb, nd))
    rs_t[...] = rsum + couple

    def block_products(x):
        k = x.shape[0] // nb
        hi, lo = split2(x)
        wide = jnp.concatenate([hi, lo, hi], axis=1)
        types = jnp.concatenate([typ_t[...]] * k, axis=0)
        out = jnp.zeros(x.shape, F32)
        for pair in range(nt // 2):
            both = dot(wide, lib_w[pair])
            out = jnp.where(types == 2 * pair, both[:, :nd], out)
            out = jnp.where(types == 2 * pair + 1, both[:, nd:], out)
        return out

    chunk = 4

    def load(ref, i):
        return ref[pl.ds(i * chunk, chunk)].reshape(chunk * nb, nd)

    def store(ref, i, value):
        ref[pl.ds(i * chunk, chunk)] = value.reshape(chunk, rl, cl, nd)

    def smooth(src, dst):
        def body(i, carry):
            v = load(src, i)
            inv = jnp.concatenate([inv_t[...]] * chunk, axis=0)
            y = v * inv
            for sweep in range(2):
                y = y + (v - block_products(y) - couple * y) * inv
            store(dst, i, y)
            return carry

        lax.fori_loop(0, sz // chunk, body, 0)

    ones = jnp.ones((8, 3 * nd), BF)

    def block_sums(src, dst):
        def body(i, carry):
            x = load(src, i)
            wide = jnp.concatenate(split3(x), axis=1)
            y = dot(ones, wide, LAST)
            for j in range(chunk):
                dst[pl.ds(i * chunk + j, 1), :] = y[0:1, j * nb : (j + 1) * nb]
            return carry

        lax.fori_loop(0, sz // chunk, body, 0)

    def put_row(own, gathered, send, recv):
        def body(off, carry):
            pltpu.make_async_remote_copy(
                src_ref=own,
                dst_ref=gathered.at[me],
                send_sem=send,
                recv_sem=recv,
                device_id=row_peer(off),
                device_id_type=MESH,
            ).start()
            return carry

        lax.fori_loop(1, n_r, body, 0)
        gathered[pl.ds(me, 1)] = own[...][None]

    def wait_bytes(gathered, sem, count):
        part = gathered.at[pl.ds(0, count)]
        pltpu.make_async_copy(part, part, sem).wait()

    block_sums(r_ref, own_rho)
    smooth(r_ref, z_ref)

    pl.semaphore_wait(barrier, n_r - 1 + n_c - 1)
    put_row(own_idt, gat_idt, send_idt, recv_idt)

    north, south = me - 1, me + 1
    west, east = mc - 1, mc + 1
    has = (me > 0, me < n_r - 1, mc > 0, mc < n_c - 1)

    def halo_copies(rnd, src):
        where = ({"row": north}, {"row": south}, {"col": west}, {"col": east})
        sources = (src.at[:, 0], src.at[:, rl - 1], edge_out.at[rnd, 0], edge_out.at[rnd, 1])
        targets = (halo_ns.at[rnd, 1], halo_ns.at[rnd, 0], halo_ew.at[rnd, 1], halo_ew.at[rnd, 0])
        landing = (halo_ns.at[rnd, 0], halo_ns.at[rnd, 1], halo_ew.at[rnd, 0], halo_ew.at[rnd, 1])
        came = (1, 0, 3, 2)
        out = []
        for k in range(4):
            give = pltpu.make_async_remote_copy(
                src_ref=sources[k],
                dst_ref=targets[k],
                send_sem=send_halo.at[rnd, k],
                recv_sem=recv_halo.at[rnd, k],
                device_id=where[k],
                device_id_type=MESH,
            )
            take = pltpu.make_async_copy(landing[k], landing[k], recv_halo.at[rnd, came[k]])
            out.append((has[k], give, take, landing[k]))
        return out

    def halo_start(rnd, src):
        edge_out[rnd, 0] = src[:, :, 0, :]
        edge_out[rnd, 1] = src[:, :, cl - 1, :]
        for here, give, _, landing in halo_copies(rnd, src):

            @pl.when(here)
            def _():
                give.start()

            @pl.when(jnp.logical_not(here))
            def _():
                landing[...] = jnp.zeros(landing.shape, F32)

    def halo_wait(rnd, src):
        for here, give, take, _ in halo_copies(rnd, src):

            @pl.when(here)
            def _():
                take.wait()
                give.wait_send()

    halo_start(0, z_ref)
    put_row(own_rho, gat_rho, send_rho, recv_rho)

    def products(src, dst):
        def body(i, carry):
            store(dst, i, block_products(load(src, i)))
            return carry

        lax.fori_loop(0, sz // chunk, body, 0)

    def lateral(rnd, src, s):
        f = src[s]
        up = halo_ns[rnd, 0, s][None]
        down = halo_ns[rnd, 1, s][None]
        fn = jnp.concatenate([up, f[:-1]], axis=0)
        fs = jnp.concatenate([f[1:], down], axis=0)
        left = halo_ew[rnd, 0, s][:, None, :]
        right = halo_ew[rnd, 1, s][:, None, :]
        fw = jnp.concatenate([left, f[:, :-1]], axis=1)
        fe = jnp.concatenate([f[:, 1:], right], axis=1)
        return strap0 * (2.0 * f - fn - fs) + strap1 * (2.0 * f - fw - fe)

    products(z_ref, u_ref)
    halo_wait(0, z_ref)

    def add_lateral(s, carry):
        u_ref[s] = u_ref[s] + lateral(0, z_ref, s)
        return carry

    lax.fori_loop(0, sz, add_lateral, 0)
    block_sums(u_ref, own_tau)
    put_row(own_tau, gat_tau, send_tau, recv_tau)

    wait_bytes(gat_idt, recv_idt, n_r - 1)
    ids = gat_idt[:, 0, :]
    typs = gat_idt[:, 1, :]
    lane = iota((n_r, nb), 1)
    dev = iota((n_r, nb), 0)
    none = jnp.full((1, nb), -1.0, F32)
    above = jnp.concatenate([none, ids[:-1]], axis=0)
    below = jnp.concatenate([ids[1:], none], axis=0)
    idsh[0] = ids
    idsh[1] = jnp.where(lane < cl, pltpu.roll(above, cl, 1), pltpu.roll(ids, cl, 1))
    idsh[2] = jnp.where(lane >= nb - cl, pltpu.roll(below, nb - cl, 1), pltpu.roll(ids, nb - cl, 1))
    idsh[3] = jnp.where(lax.rem(lane, cl) == 0, -1.0, pltpu.roll(ids, 1, 1))
    idsh[4] = jnp.where(lax.rem(lane, cl) == cl - 1, -1.0, pltpu.roll(ids, nb - 1, 1))
    centre = jnp.zeros((n_r, nb), F32)
    for t in range(nt):
        centre = jnp.where(typs == t, sums[t], centre)
    idsh[5] = centre + 2.0 * nw + 2.0 * ew

    acc[...] = jnp.zeros(acc.shape, F32)
    dacc[...] = jnp.zeros(dacc.shape, F32)
    agg = iota((ng, 2 * nb), 0).astype(F32)

    def assemble(k, carry):
        def pair(j):
            return jnp.concatenate(
                [idsh[j, pl.ds(2 * k, 1), :], idsh[j, pl.ds(2 * k + 1, 1), :]], axis=1
            )

        here = agg == pair(0)
        mask = onehot(here)
        oh_all[k] = mask
        other = jnp.concatenate([onehot(agg == pair(2)), onehot(agg == pair(4))], axis=0)
        acc[...] += dot(mask, other, LAST)
        weighted = jnp.where(here, pair(5), 0.0)
        dacc[...] += weighted[:, :nb] + weighted[:, nb:]
        return carry

    lax.fori_loop(0, n_r // 2, assemble, 0)
    big_eye = iota((ng, ng), 0) == iota((ng, ng), 1)
    cross = nw * acc[:, :ng] + ew * acc[:, ng:]
    total = jnp.sum(dacc[...], axis=1, keepdims=True)
    coarse = jnp.where(big_eye, total, 0.0) - cross - jnp.transpose(cross)
    on_diag = jnp.where(big_eye, coarse, 0.0)
    scale = lax.rsqrt(jnp.sum(on_diag, axis=0, keepdims=True))
    scaled = coarse * scale * lax.rsqrt(jnp.sum(on_diag, axis=1, keepdims=True))
    a_hi, a_mid, a_lo = split3(scaled)
    mat[0] = a_hi
    mat[1] = a_mid
    mat[2] = a_lo
    mat_h[:, 0:ng] = a_hi
    mat_h[:, ng : 2 * ng] = a_mid
    mat_h[:, 2 * ng : 3 * ng] = a_hi

    low = jnp.broadcast_to(0.0085 * ew / (nw + ew), (1, ng))
    mu = 2.0 / (1.0 + low)
    xmat[...] = jnp.where(big_eye, mu, 0.0) - (0.25 * mu * mu) * scaled
    low = 4.0 * low / ((1.0 + low) * (1.0 + low))

    def newton(i, low):
        mu = 2.0 / (1.0 + low)
        x = xmat[...]
        x_hi, x_lo = split2(x)
        t_hi, t_lo = split2(dot(mat_h[...], jnp.concatenate([x_hi, x_hi, x_lo], axis=0)))
        xt = dot(
            jnp.concatenate([x_hi, x_lo, x_hi], axis=1),
            jnp.concatenate([t_hi, t_hi, t_lo], axis=0),
        )
        xmat[...] = 2.0 * mu * x - (mu * mu) * xt
        return 4.0 * low / ((1.0 + low) * (1.0 + low))

    lax.fori_loop(0, NEWTON, newton, low)
    inv_hi, inv_lo = split2(xmat[...])

    def by_inverse(g):
        y = dot(jnp.concatenate(split2(g), axis=0), inv_hi)
        return y[:sz] + y[sz:] + dot(g.astype(BF), inv_lo)

    def by_matrix(c):
        c_hi, c_mid, c_lo = split3(c)
        y = dot(jnp.concatenate([c_hi, c_mid, c_lo], axis=0), mat[0])
        x = dot(jnp.concatenate([c_hi, c_mid], axis=0), mat[1])
        return (y[2 * sz :] + x[sz:] + dot(c_hi, mat[2])) + (y[sz : 2 * sz] + x[:sz]) + y[:sz]

    def solve(g):
        g = g * scale
        c = by_inverse(g)
        for _ in range(REFINE):
            c = c + by_inverse(g - by_matrix(c))
        return c * scale

    def aggregate(gathered):
        def body(k, total):
            x = jnp.concatenate([gathered[2 * k], gathered[2 * k + 1]], axis=1)
            return total + rows_dot(x, oh_all[k], LAST)

        return lax.fori_loop(0, n_r // 2, body, jnp.zeros((sz, ng), F32))

    wait_bytes(gat_rho, recv_rho, n_r - 1)
    sums_r = aggregate(gat_rho)
    c = solve(sums_r)

    pick = iota((nb, nb), 0)
    slot = iota((nb, nb), 1)
    first = dot(ids.astype(BF), onehot(pick == slot * cl))
    final = dot(ids.astype(BF), onehot(pick == slot * cl + cl - 1))
    agg_lane = iota((n_r, ng), 1).astype(F32)
    oh_first = jnp.concatenate([onehot(first[:, j : j + 1] == agg_lane) for j in range(rl)], axis=0)
    oh_final = jnp.concatenate([onehot(final[:, j : j + 1] == agg_lane) for j in range(rl)], axis=0)
    cedge_out[0] = rows_dot(c, oh_first, LAST)
    cedge_out[1] = rows_dot(c, oh_final, LAST)

    def edge_copies():
        out = []
        for k, to in ((0, west), (1, east)):
            give = pltpu.make_async_remote_copy(
                src_ref=cedge_out.at[k],
                dst_ref=cedge_in.at[1 - k],
                send_sem=send_edge.at[k],
                recv_sem=recv_edge.at[k],
                device_id={"col": to},
                device_id_type=MESH,
            )
            take = pltpu.make_async_copy(cedge_in.at[k], cedge_in.at[k], recv_edge.at[1 - k])
            out.append((has[2 + k], give, take, cedge_in.at[k]))
        return out

    for here, give, _, landing in edge_copies():

        @pl.when(here)
        def _():
            give.start()

        @pl.when(jnp.logical_not(here))
        def _():
            landing[...] = jnp.zeros(landing.shape, F32)

    wide_lane = iota((nb, ng), 1).astype(F32)

    def local_onehot(j):
        col = column(idsh[j, pl.ds(me, 1), :])
        return jnp.concatenate([col] * (ng // nb), axis=1) == wide_lane

    oh_own = onehot(local_onehot(0))
    oh_ns = onehot(local_onehot(1)) + onehot(local_onehot(2))
    oh_we = onehot(local_onehot(3)) + onehot(local_onehot(4))
    c_own = cols_dot(oh_own, c)
    c_ns = cols_dot(oh_ns, c)
    c_we = cols_dot(oh_we, c)
    wait_bytes(gat_tau, recv_tau, n_r - 1)
    sums_u = aggregate(gat_tau) + sums_r

    for here, give, take, _ in edge_copies():

        @pl.when(here)
        def _():
            take.wait()
            give.wait_send()

    block = iota((nb, ng), 0)
    spot = iota((nb, ng), 1) == (block // cl) * n_r + me
    at_west = onehot(jnp.logical_and(lax.rem(block, cl) == 0, spot))
    at_east = onehot(jnp.logical_and(lax.rem(block, cl) == cl - 1, spot))
    from_west = cedge_in[0]
    from_east = cedge_in[1]
    c_we = c_we + cols_dot(at_west, from_west) + cols_dot(at_east, from_east)
    over = rows_dot(from_west, oh_first, PLAIN) + rows_dot(from_east, oh_final, PLAIN)
    d = solve(sums_u - ew * over)
    d_own = cols_dot(oh_own, d)

    rs = rs_t[...]
    for s in range(sz):
        own = c_own[:, s : s + 1]
        image = own * rs - c_ns[:, s : s + 1] * strap0 - c_we[:, s : s + 1] * strap1
        z_ref[s] = z_ref[s] + jnp.broadcast_to(own, (nb, nd)).reshape(rl, cl, nd)
        u_ref[s] = u_ref[s] + image.reshape(rl, cl, nd)

    smooth(u_ref, w_ref)
    for s in range(sz):
        w_ref[s] = w_ref[s] + jnp.broadcast_to(d_own[:, s : s + 1], (nb, nd)).reshape(rl, cl, nd)
    halo_start(1, w_ref)
    products(w_ref, t_ref)
    halo_wait(1, w_ref)

    def finish(s, carry):
        r, z, u, w = r_ref[s], z_ref[s], u_ref[s], w_ref[s]
        t = t_ref[s] + lateral(1, w_ref, s)
        t_ref[s] = t
        for k, (a, b) in enumerate(((r, z), (z, u), (r, w), (u, w), (z, t), (w, t))):
            part = jnp.sum((a * b).reshape(nb, nd), axis=0, keepdims=True)
            dots[k, pl.ds(s, 1), :] = part
        return carry

    lax.fori_loop(0, sz, finish, 0)

    lane_s = iota((sz, nd), 1)
    row_s = iota((sz, nd), 0)
    packed = jnp.zeros((sz, nd), F32)
    for k in range(6):
        value = jnp.sum(dots[k], axis=1, keepdims=True)
        packed = packed + jnp.where(lane_s == row_s * 8 + k, value, 0.0)
    own_sum[...] = jnp.sum(packed, axis=0, keepdims=True)
    put_row(own_sum, row_sum, send_rs, recv_rs)
    wait_bytes(row_sum, recv_rs, n_r - 1)
    own_col[...] = jnp.sum(row_sum[...], axis=0)

    def put_col(off, carry):
        pltpu.make_async_remote_copy(
            src_ref=own_col,
            dst_ref=col_sum.at[mc],
            send_sem=send_cs,
            recv_sem=recv_cs,
            device_id=col_peer(off),
            device_id_type=MESH,
        ).start()
        return carry

    lax.fori_loop(1, n_c, put_col, 0)
    col_sum[pl.ds(mc, 1)] = own_col[...][None]
    wait_bytes(col_sum, recv_cs, n_c - 1)
    every = jnp.broadcast_to(jnp.sum(col_sum[...], axis=0), (sz, nd))

    def unpack(k):
        return jnp.sum(jnp.where(lane_s == row_s * 8 + k, every, 0.0), axis=1, keepdims=True)

    rz, zu, rw, uw, zt, wt = [unpack(k) for k in range(6)]
    step0 = rz / zu
    fresh = rz - step0 * (rw + zu) + step0 * step0 * uw
    blend1 = 1.0 + fresh / rz
    curv = blend1 * blend1 * zu - blend1 * step0 * (zt + uw) + step0 * step0 * wt
    step1 = fresh / curv
    on_first = step0 + step1 * blend1
    on_second = step0 * step1
    dots[0] = jnp.broadcast_to(on_first, (sz, nd))
    dots[1] = jnp.broadcast_to(on_second, (sz, nd))

    def output(s, carry):
        a = dots[0, pl.ds(s, 1), :]
        b = dots[1, pl.ds(s, 1), :]
        v_ref[s] = a * z_ref[s] - b * w_ref[s]
        res_ref[s] = r_ref[s] - a * u_ref[s] + b * t_ref[s]
        return carry

    lax.fori_loop(0, sz, output, 0)

    wait_bytes(gat_idt, send_idt, n_r - 1)
    wait_bytes(gat_rho, send_rho, n_r - 1)
    wait_bytes(gat_tau, send_tau, n_r - 1)
    wait_bytes(row_sum, send_rs, n_r - 1)
    wait_bytes(col_sum, send_cs, n_c - 1)


def on_device(n_r, n_c, load_currents, block_library, strap_conductance, block_types, aggregate_map):
    sz, rl, cl, nd = load_currents.shape
    nt = block_library.shape[0]
    nb = rl * cl
    ng = n_r * rl // AGR * (cl // AGC)
    vmem = pl.BlockSpec(memory_space=pltpu.VMEM)
    field = pltpu.VMEM((sz, rl, cl, nd), F32)
    shape = jax.ShapeDtypeStruct(load_currents.shape, F32)
    dma = pltpu.SemaphoreType.DMA
    table = pltpu.VMEM((nb, nd), F32)
    return pl.pallas_call(
        functools.partial(kernel, n_r, n_c),
        out_shape=(shape, shape),
        in_specs=[vmem] * 5,
        out_specs=(vmem, vmem),
        scratch_shapes=[
            field, field, field, field,
            pltpu.VMEM((nt // 2, 3 * nd, 2 * nd), BF), table, table, table, table,
            pltpu.VMEM((2, nb), F32), pltpu.VMEM((n_r, 2, nb), F32),
            pltpu.VMEM((sz, nb), F32), pltpu.VMEM((n_r, sz, nb), F32),
            pltpu.VMEM((sz, nb), F32), pltpu.VMEM((n_r, sz, nb), F32),
            pltpu.VMEM((6, n_r, nb), F32), pltpu.VMEM((n_r // 2, ng, 2 * nb), BF),
            pltpu.VMEM((ng, 2 * ng), F32), pltpu.VMEM((ng, nb), F32),
            pltpu.VMEM((3, ng, ng), BF), pltpu.VMEM((ng, 3 * ng), BF), pltpu.VMEM((ng, ng), F32),
            pltpu.VMEM((2, 2, sz, rl, nd), F32), pltpu.VMEM((2, 2, sz, cl, nd), F32),
            pltpu.VMEM((2, 2, sz, rl, nd), F32),
            pltpu.VMEM((2, sz, ng), F32), pltpu.VMEM((2, sz, ng), F32),
            pltpu.VMEM((6, sz, nd), F32), pltpu.VMEM((1, nd), F32), pltpu.VMEM((n_r, 1, nd), F32),
            pltpu.VMEM((1, nd), F32), pltpu.VMEM((n_c, 1, nd), F32),
            dma, dma, dma, dma, dma, dma,
            dma((2, 4)), dma((2, 4)), dma((2,)), dma((2,)),
            dma, dma, dma, dma,
        ],
        compiler_params=pltpu.CompilerParams(
            collective_id=0, has_side_effects=True, vmem_limit_bytes=56 * 1024 * 1024
        ),
    )(load_currents, block_library, strap_conductance, block_types, aggregate_map)


def solution(mesh):
    placed = (P(None, "row", "col", None), P(), P(), P("row", "col"), P("row", "col"))
    return jax.shard_map(
        functools.partial(on_device, mesh.shape["row"], mesh.shape["col"]),
        mesh=mesh,
        in_specs=placed,
        out_specs=(P(None, "row", "col", None), P(None, "row", "col", None)),
        check_vma=False,
    )
```

```python
import functools
import jax
import jax.numpy as jnp
from jax import lax
from jax.experimental import pallas as pl
from jax.experimental.pallas import tpu as pltpu
from jax.sharding import PartitionSpec as P

MESH = pl.DeviceIdType.MESH
F32 = jnp.float32
BF = jnp.bfloat16
LAST = (((1,), (1,)), ((), ()))
PLAIN = (((1,), (0,)), ((), ()))
NEWTON = 6
REFINE = 2
AGR = 4
AGC = 4
GROUP = 8
UNROLL = 4
STEP = 4


def iota(shape, dim):
    return lax.broadcasted_iota(jnp.int32, shape, dim)


def onehot(mask):
    return jnp.where(mask, 1.0, 0.0).astype(BF)


def split2(x):
    hi = x.astype(BF)
    lo = (x - hi.astype(F32)).astype(BF)
    return hi, lo


def split3(x):
    hi = x.astype(BF)
    rest = x - hi.astype(F32)
    mid = rest.astype(BF)
    lo = (rest - mid.astype(F32)).astype(BF)
    return hi, mid, lo


def dot(a, b, dims=PLAIN):
    return lax.dot_general(a, b, dims, preferred_element_type=F32)


def rows_dot(x, table, dims):
    m = x.shape[0]
    y = dot(jnp.concatenate(split3(x), axis=0), table, dims)
    return y[:m] + y[m : 2 * m] + y[2 * m :]


def cols_dot(table, x):
    m = x.shape[0]
    y = dot(table, jnp.concatenate(split3(x), axis=0), LAST)
    return y[:, :m] + y[:, m : 2 * m] + y[:, 2 * m :]


def flat_row(ref, rl, cl):
    nb = rl * cl
    spread = onehot(iota((cl, nb), 0) == lax.rem(iota((cl, nb), 1), cl))
    mine = iota((rl, nb), 0) == iota((rl, nb), 1) // cl
    wide = dot(ref[...].astype(F32).astype(BF), spread)
    return jnp.sum(jnp.where(mine, wide, 0.0), axis=0, keepdims=True)


def order_kernel(nt, typ_ref, idx_v):
    rl, cl = typ_ref.shape
    nb = rl * cl
    typ_row = flat_row(typ_ref, rl, cl)

    one_type = iota((nt, nb), 0).astype(F32) == typ_row
    before = dot(onehot(one_type), onehot(iota((nb, nb), 0) < iota((nb, nb), 1)))
    members = jnp.sum(jnp.where(one_type, 1.0, 0.0), axis=1, keepdims=True)
    groups = jnp.floor((members + (GROUP - 1)) * (1.0 / GROUP))
    start = jnp.zeros((1, 1), F32)
    slot_row = jnp.zeros((1, nb), F32)
    group_lane = iota((1, 2 * nb), 1).astype(F32)
    group_type = jnp.zeros((1, 2 * nb), F32)
    for t in range(nt):
        slot_row = jnp.where(typ_row == t, GROUP * start + before[t : t + 1], slot_row)
        start = start + groups[t : t + 1]
        if t < nt - 1:
            group_type = group_type + jnp.where(start <= group_lane, 1.0, 0.0)
    slot_col = jnp.transpose(jnp.broadcast_to(slot_row, (nb, nb)))
    holds = onehot(jnp.concatenate([slot_col, slot_col], axis=1) == iota((nb, 2 * nb), 1).astype(F32))
    number = iota((8, nb), 1).astype(F32).astype(BF)
    idx_v[...] = jnp.zeros(idx_v.shape, jnp.int32)
    idx_v[0:1, :] = dot(number, holds)[0:1].astype(jnp.int32)
    idx_v[1:2, :] = jnp.concatenate([slot_row, slot_row], axis=1).astype(jnp.int32)
    idx_v[2:3, :] = group_type.astype(jnp.int32)


def kernel(
    n_r, n_c, rl, cl,
    r_ref, lib_ref, strap_ref, typ_ref, ids_ref, typ_s, idx_s,
    v_ref, res_ref,
    z_ref, w_ref, u_ref, t_ref, rb_ref, sorted_y, sorted_p,
    lib_w, inv_l, rs_l,
    own_idt, gat_idt, own_rho, gat_rho, own_tau, gat_tau,
    idsh, oh_all, acc, dacc, mat, mat_h, xmat,
    cedge_out, cedge_in, coarse_b,
    dots, own_sum, row_sum, own_col, col_sum,
    send_idt, recv_idt, send_rho, recv_rho, send_tau, recv_tau,
    send_halo, recv_halo, send_edge, recv_edge,
    send_rs, recv_rs, send_cs, recv_cs, load_sem,
):
    nt, nd, _ = lib_ref.shape
    nb = rl * cl
    sz = r_ref.shape[0]
    ng = acc.shape[0]
    slots = sorted_y.shape[0]
    me = lax.axis_index("row")
    mc = lax.axis_index("col")

    def row_peer(off):
        return {"row": lax.rem(me + off, n_r)}

    def col_peer(off):
        return {"col": lax.rem(mc + off, n_c)}

    barrier = pltpu.get_barrier_semaphore()

    def greet_row(off, carry):
        pl.semaphore_signal(barrier, inc=1, device_id=row_peer(off), device_id_type=MESH)
        return carry

    def greet_col(off, carry):
        pl.semaphore_signal(barrier, inc=1, device_id=col_peer(off), device_id_type=MESH)
        return carry

    load_copies = [pltpu.make_async_copy(r_ref.at[s], rb_ref.at[:, s], load_sem) for s in range(sz)]
    for copy in load_copies:
        copy.start()
    lax.fori_loop(1, n_r, greet_row, 0)
    lax.fori_loop(1, n_c, greet_col, 0)

    strap0 = strap_ref[0:1, :]
    strap1 = strap_ref[1:2, :]
    couple = 2.0 * strap0 + 2.0 * strap1
    nw = jnp.sum(strap0, axis=1, keepdims=True)
    ew = jnp.sum(strap1, axis=1, keepdims=True)
    eye = iota((nd, nd), 0) == iota((nd, nd), 1)
    id_row = flat_row(ids_ref, rl, cl)
    typ_row = flat_row(typ_ref, rl, cl)
    own_idt[0:1, :] = id_row
    own_idt[1:2, :] = typ_row

    sums = []
    for t in range(nt):
        lib = lib_ref[t]
        hi, lo = split2(lib)
        lib_w[t, 0:nd, 0:nd] = hi
        lib_w[t, nd : 2 * nd, 0:nd] = hi
        lib_w[t, 0:nd, nd : 2 * nd] = lo
        lib_w[t, nd : 2 * nd, nd : 2 * nd] = lo
        rows = jnp.sum(lib, axis=0, keepdims=True)
        sums.append(jnp.sum(rows, axis=1, keepdims=True))
        rs_l[t : t + 1, :] = rows
        inv_l[t : t + 1, :] = 1.0 / (jnp.sum(jnp.where(eye, lib, 0.0), axis=0, keepdims=True) + couple)

    def block_products(y, lib):
        both = dot(jnp.concatenate(split2(y), axis=1), lib)
        return both[:, :nd] + both[:, nd:]

    def smooth(load):
        def body(i, carry):
            for q in range(UNROLL):
                g = i * UNROLL + q
                kind = idx_s[2, g]
                lib = lib_w[kind]
                inv = inv_l[pl.ds(kind, 1), :]
                v = jnp.concatenate([load(idx_s[0, g * GROUP + j]) for j in range(GROUP)], axis=0)
                y = v * inv
                for sweep in range(2):
                    y = y + (v - block_products(y, lib) - couple * y) * inv
                sorted_y[pl.ds(g * GROUP, GROUP)] = y.reshape(GROUP, sz, nd)
                p = block_products(y, lib)
                sorted_p[pl.ds(g * GROUP, GROUP)] = p.reshape(GROUP, sz, nd)
            return carry

        lax.fori_loop(0, slots // (GROUP * UNROLL), body, 0)

    lane_b = iota((sz, nb), 1)

    def put_row(own, gathered, send, recv):
        def body(off, carry):
            pltpu.make_async_remote_copy(
                src_ref=own,
                dst_ref=gathered.at[me],
                send_sem=send,
                recv_sem=recv,
                device_id=row_peer(off),
                device_id_type=MESH,
            ).start()
            return carry

        lax.fori_loop(1, n_r, body, 0)
        gathered[pl.ds(me, 1)] = own[...][None]

    def wait_bytes(gathered, sem, count):
        part = gathered.at[pl.ds(0, count)]
        pltpu.make_async_copy(part, part, sem).wait()

    def regroup(r, rho):
        for c in range(cl):
            b = r * cl + c
            rho = jnp.where(lane_b == b, jnp.sum(rb_ref[b], axis=1, keepdims=True), rho)
        return rho

    pltpu.make_async_copy(rb_ref, rb_ref, load_sem).wait()
    own_rho[...] = lax.fori_loop(0, rl, regroup, jnp.zeros((sz, nb), F32))

    pl.semaphore_wait(barrier, n_r - 1 + n_c - 1)
    put_row(own_idt, gat_idt, send_idt, recv_idt)
    put_row(own_rho, gat_rho, send_rho, recv_rho)

    smooth(lambda b: rb_ref[b])

    north, south = me - 1, me + 1
    west, east = mc - 1, mc + 1
    has = (me > 0, me < n_r - 1, mc > 0, mc < n_c - 1)

    def halo_copies(rnd, field):
        where = ({"row": north}, {"row": south}, {"col": west}, {"col": east})
        inner_r, inner_c = pl.ds(1, rl), pl.ds(1, cl)
        sources = (field.at[1, inner_c], field.at[rl, inner_c], field.at[inner_r, 1], field.at[inner_r, cl])
        landing = (
            field.at[0, inner_c], field.at[rl + 1, inner_c], field.at[inner_r, 0], field.at[inner_r, cl + 1]
        )
        opposite = (1, 0, 3, 2)
        out = []
        for k in range(4):
            give = pltpu.make_async_remote_copy(
                src_ref=sources[k],
                dst_ref=landing[opposite[k]],
                send_sem=send_halo.at[rnd, k],
                recv_sem=recv_halo.at[rnd, k],
                device_id=where[k],
                device_id_type=MESH,
            )
            take = pltpu.make_async_copy(landing[k], landing[k], recv_halo.at[rnd, opposite[k]])
            out.append((has[k], give, take, landing[k]))
        return out

    def halo_start(rnd, field):
        for here, give, _, landing in halo_copies(rnd, field):

            @pl.when(here)
            def _():
                give.start()

            @pl.when(jnp.logical_not(here))
            def _():
                landing[...] = jnp.zeros(landing.shape, F32)

    def halo_wait(rnd, field):
        for here, give, take, _ in halo_copies(rnd, field):

            @pl.when(here)
            def _():
                take.wait()
                give.wait_send()

    def place_s(r, carry):
        for c in range(cl):
            z_ref[r + 1, c + 1] = sorted_y[idx_s[1, r * cl + c]]
        return carry

    lax.fori_loop(0, rl, place_s, 0)
    halo_start(0, z_ref)

    def lateral(field, r, c):
        f = field[r + 1, c + 1]
        fn = field[r, c + 1]
        fs = field[r + 2, c + 1]
        fw = field[r + 1, c]
        fe = field[r + 1, c + 2]
        return strap0 * (2.0 * f - fn - fs) + strap1 * (2.0 * f - fw - fe)

    halo_wait(0, z_ref)

    def image_s(r, tau):
        for c in range(cl):
            b = r * cl + c
            u = sorted_p[idx_s[1, b]] + lateral(z_ref, r, c)
            u_ref[b] = u
            tau = jnp.where(lane_b == b, jnp.sum(u, axis=1, keepdims=True), tau)
        return tau

    own_tau[...] = lax.fori_loop(0, rl, image_s, jnp.zeros((sz, nb), F32))
    put_row(own_tau, gat_tau, send_tau, recv_tau)

    wait_bytes(gat_idt, recv_idt, n_r - 1)
    ids = gat_idt[:, 0, :]
    typs = gat_idt[:, 1, :]
    lane = iota((n_r, nb), 1)
    none = jnp.full((1, nb), -1.0, F32)
    above = jnp.concatenate([none, ids[:-1]], axis=0)
    below = jnp.concatenate([ids[1:], none], axis=0)
    idsh[0] = ids
    idsh[1] = jnp.where(lane < cl, pltpu.roll(above, cl, 1), pltpu.roll(ids, cl, 1))
    idsh[2] = jnp.where(lane >= nb - cl, pltpu.roll(below, nb - cl, 1), pltpu.roll(ids, nb - cl, 1))
    idsh[3] = jnp.where(lax.rem(lane, cl) == 0, -1.0, pltpu.roll(ids, 1, 1))
    idsh[4] = jnp.where(lax.rem(lane, cl) == cl - 1, -1.0, pltpu.roll(ids, nb - 1, 1))
    centre = jnp.zeros((n_r, nb), F32)
    for t in range(nt):
        centre = jnp.where(typs == t, sums[t], centre)
    idsh[5] = centre + 2.0 * nw + 2.0 * ew

    acc[...] = jnp.zeros(acc.shape, F32)
    dacc[...] = jnp.zeros(dacc.shape, F32)
    agg = iota((ng, STEP * nb), 0).astype(F32)

    def assemble(k, carry):
        def several(j):
            return jnp.concatenate([idsh[j, pl.ds(STEP * k + i, 1), :] for i in range(STEP)], axis=1)

        here = agg == several(0)
        mask = onehot(here)
        oh_all[k] = mask
        other = jnp.concatenate([onehot(agg == several(2)), onehot(agg == several(4))], axis=0)
        acc[...] += dot(mask, other, LAST)
        weighted = jnp.where(here, several(5), 0.0)
        more = weighted[:, :nb]
        for i in range(1, STEP):
            more = more + weighted[:, i * nb : (i + 1) * nb]
        dacc[...] += more
        return carry

    lax.fori_loop(0, n_r // STEP, assemble, 0)
    big_eye = iota((ng, ng), 0) == iota((ng, ng), 1)
    cross = nw * acc[:, :ng] + ew * acc[:, ng:]
    total = jnp.sum(dacc[...], axis=1, keepdims=True)
    coarse = jnp.where(big_eye, total, 0.0) - cross - jnp.transpose(cross)
    on_diag = jnp.where(big_eye, coarse, 0.0)
    scale = lax.rsqrt(jnp.sum(on_diag, axis=0, keepdims=True))
    scaled = coarse * scale * lax.rsqrt(jnp.sum(on_diag, axis=1, keepdims=True))
    a_hi, a_mid, a_lo = split3(scaled)
    mat[0] = a_hi
    mat[1] = a_mid
    mat[2] = a_lo
    mat_h[:, 0:ng] = a_hi
    mat_h[:, ng : 2 * ng] = a_mid
    mat_h[:, 2 * ng : 3 * ng] = a_hi

    low = jnp.broadcast_to(0.0085 * ew / (nw + ew), (1, ng))
    mu = 2.0 / (1.0 + low)
    xmat[...] = jnp.where(big_eye, mu, 0.0) - (0.25 * mu * mu) * scaled
    low = 4.0 * low / ((1.0 + low) * (1.0 + low))

    def newton(i, low):
        mu = 2.0 / (1.0 + low)
        x = xmat[...]
        x_hi, x_lo = split2(x)
        t_hi, t_lo = split2(dot(mat_h[...], jnp.concatenate([x_hi, x_hi, x_lo], axis=0)))
        xt = dot(
            jnp.concatenate([x_hi, x_lo, x_hi], axis=1),
            jnp.concatenate([t_hi, t_hi, t_lo], axis=0),
        )
        xmat[...] = 2.0 * mu * x - (mu * mu) * xt
        return 4.0 * low / ((1.0 + low) * (1.0 + low))

    lax.fori_loop(0, NEWTON, newton, low)
    inv_hi, inv_lo = split2(xmat[...])

    def by_inverse(g):
        y = dot(jnp.concatenate(split2(g), axis=0), inv_hi)
        return y[:sz] + y[sz:] + dot(g.astype(BF), inv_lo)

    def by_matrix(c):
        c_hi, c_mid, c_lo = split3(c)
        y = dot(jnp.concatenate([c_hi, c_mid, c_lo], axis=0), mat[0])
        x = dot(jnp.concatenate([c_hi, c_mid], axis=0), mat[1])
        return (y[2 * sz :] + x[sz:] + dot(c_hi, mat[2])) + (y[sz : 2 * sz] + x[:sz]) + y[:sz]

    def solve(g):
        g = g * scale
        c = by_inverse(g)
        for _ in range(REFINE):
            c = c + by_inverse(g - by_matrix(c))
        return c * scale

    def aggregate(gathered):
        def body(k, total):
            x = jnp.concatenate([gathered[STEP * k + i] for i in range(STEP)], axis=1)
            return total + rows_dot(x, oh_all[k], LAST)

        return lax.fori_loop(0, n_r // STEP, body, jnp.zeros((sz, ng), F32))

    wait_bytes(gat_rho, recv_rho, n_r - 1)
    sums_r = aggregate(gat_rho)
    c = solve(sums_r)

    pick = iota((nb, nb), 0)
    slot = iota((nb, nb), 1)
    first = dot(ids.astype(BF), onehot(pick == slot * cl))
    final = dot(ids.astype(BF), onehot(pick == slot * cl + cl - 1))
    agg_lane = iota((n_r, ng), 1).astype(F32)
    oh_first = jnp.concatenate([onehot(first[:, j : j + 1] == agg_lane) for j in range(rl)], axis=0)
    oh_final = jnp.concatenate([onehot(final[:, j : j + 1] == agg_lane) for j in range(rl)], axis=0)
    cedge_out[0] = rows_dot(c, oh_first, LAST)
    cedge_out[1] = rows_dot(c, oh_final, LAST)

    def edge_copies():
        out = []
        for k, to in ((0, west), (1, east)):
            give = pltpu.make_async_remote_copy(
                src_ref=cedge_out.at[k],
                dst_ref=cedge_in.at[1 - k],
                send_sem=send_edge.at[k],
                recv_sem=recv_edge.at[k],
                device_id={"col": to},
                device_id_type=MESH,
            )
            take = pltpu.make_async_copy(cedge_in.at[k], cedge_in.at[k], recv_edge.at[1 - k])
            out.append((has[2 + k], give, take, cedge_in.at[k]))
        return out

    for here, give, _, landing in edge_copies():

        @pl.when(here)
        def _():
            give.start()

        @pl.when(jnp.logical_not(here))
        def _():
            landing[...] = jnp.zeros(landing.shape, F32)

    tall = iota((ng, nb), 0).astype(F32)

    def local_onehot(j):
        return onehot(tall == idsh[j, pl.ds(me, 1), :])

    oh_own = local_onehot(0)
    oh_we = local_onehot(3) + local_onehot(4)
    oh_own_ns = jnp.concatenate([oh_own, local_onehot(1) + local_onehot(2)], axis=1)
    c_own_ns = rows_dot(c, oh_own_ns, PLAIN)
    coarse_b[0] = c_own_ns[:, 0:nb]
    coarse_b[1] = c_own_ns[:, nb:]
    coarse_b[2] = rows_dot(c, oh_we, PLAIN)
    wait_bytes(gat_tau, recv_tau, n_r - 1)
    sums_u = aggregate(gat_tau) + sums_r

    for here, give, take, _ in edge_copies():

        @pl.when(here)
        def _():
            take.wait()
            give.wait_send()

    block = iota((ng, nb), 1)
    spot = iota((ng, nb), 0) == (block // cl) * n_r + me
    at_west = onehot(jnp.logical_and(lax.rem(block, cl) == 0, spot))
    at_east = onehot(jnp.logical_and(lax.rem(block, cl) == cl - 1, spot))
    from_west = cedge_in[0]
    from_east = cedge_in[1]
    at_sides = jnp.concatenate([at_west, at_east], axis=1)
    coarse_b[2] = (
        coarse_b[2] + rows_dot(from_west, at_sides, PLAIN)[:, :nb] + rows_dot(from_east, at_sides, PLAIN)[:, nb:]
    )
    over = rows_dot(from_west, oh_first, PLAIN) + rows_dot(from_east, oh_final, PLAIN)
    d = solve(sums_u - ew * over)
    coarse_b[3] = rows_dot(d, oh_own_ns, PLAIN)[:, :nb]

    def turned(j, r):
        return pltpu.roll(coarse_b[j], lax.rem(nb - r * cl, nb), 1)

    def apply_c(r, carry):
        own, ns, we = turned(0, r), turned(1, r), turned(2, r)
        for c in range(cl):
            b = r * cl + c
            rs = rs_l[pl.ds(typ_s[r, c], 1), :] + couple
            mid = own[:, c : c + 1]
            z_ref[r + 1, c + 1] += jnp.broadcast_to(mid, (sz, nd))
            u_ref[b] += mid * rs - ns[:, c : c + 1] * strap0 - we[:, c : c + 1] * strap1
        return carry

    lax.fori_loop(0, rl, apply_c, 0)
    smooth(lambda b: u_ref[b])

    def place_w(r, carry):
        extra = turned(3, r)
        for c in range(cl):
            w_ref[r + 1, c + 1] = sorted_y[idx_s[1, r * cl + c]] + extra[:, c : c + 1]
        return carry

    lax.fori_loop(0, rl, place_w, 0)
    halo_start(1, w_ref)
    halo_wait(1, w_ref)

    def finish(row, parts):
        extra = turned(3, row)
        for c in range(cl):
            b = row * cl + c
            rs = rs_l[pl.ds(typ_s[row, c], 1), :]
            t = sorted_p[idx_s[1, b]] + extra[:, c : c + 1] * rs + lateral(w_ref, row, c)
            t_ref[b] = t
            r, z, u, w = rb_ref[b], z_ref[row + 1, c + 1], u_ref[b], w_ref[row + 1, c + 1]
            pairs = ((r, z), (z, u), (r, w), (u, w), (z, t), (w, t))
            parts = tuple(p + x * y for p, (x, y) in zip(parts, pairs))
        return parts

    parts = lax.fori_loop(0, rl, finish, tuple(jnp.zeros((sz, nd), F32) for _ in range(6)))

    lane_s = iota((sz, nd), 1)
    row_s = iota((sz, nd), 0)
    packed = jnp.zeros((sz, nd), F32)
    for k in range(6):
        value = jnp.sum(parts[k], axis=1, keepdims=True)
        packed = packed + jnp.where(lane_s == row_s * 8 + k, value, 0.0)
    own_sum[...] = jnp.sum(packed, axis=0, keepdims=True)
    put_row(own_sum, row_sum, send_rs, recv_rs)
    wait_bytes(row_sum, recv_rs, n_r - 1)
    own_col[...] = jnp.sum(row_sum[...], axis=0)

    def put_col(off, carry):
        pltpu.make_async_remote_copy(
            src_ref=own_col,
            dst_ref=col_sum.at[mc],
            send_sem=send_cs,
            recv_sem=recv_cs,
            device_id=col_peer(off),
            device_id_type=MESH,
        ).start()
        return carry

    lax.fori_loop(1, n_c, put_col, 0)
    col_sum[pl.ds(mc, 1)] = own_col[...][None]
    wait_bytes(col_sum, recv_cs, n_c - 1)
    every = jnp.broadcast_to(jnp.sum(col_sum[...], axis=0), (sz, nd))

    def unpack(k):
        return jnp.sum(jnp.where(lane_s == row_s * 8 + k, every, 0.0), axis=1, keepdims=True)

    rz, zu, rw, uw, zt, wt = [unpack(k) for k in range(6)]
    step0 = rz / zu
    fresh = rz - step0 * (rw + zu) + step0 * step0 * uw
    blend1 = 1.0 + fresh / rz
    curv = blend1 * blend1 * zu - blend1 * step0 * (zt + uw) + step0 * step0 * wt
    step1 = fresh / curv
    on_first = jnp.broadcast_to(step0 + step1 * blend1, (sz, nd))
    on_second = jnp.broadcast_to(step0 * step1, (sz, nd))

    def output(r, carry):
        for c in range(cl):
            b = r * cl + c
            v_ref[b] = on_first * z_ref[r + 1, c + 1] - on_second * w_ref[r + 1, c + 1]
            res_ref[b] = rb_ref[b] - on_first * u_ref[b] + on_second * t_ref[b]
        return carry

    lax.fori_loop(0, rl, output, 0)

    wait_bytes(gat_idt, send_idt, n_r - 1)
    wait_bytes(gat_rho, send_rho, n_r - 1)
    wait_bytes(gat_tau, send_tau, n_r - 1)
    wait_bytes(row_sum, send_rs, n_r - 1)
    wait_bytes(col_sum, send_cs, n_c - 1)


def on_device(n_r, n_c, load_currents, block_library, strap_conductance, block_types, aggregate_map):
    sz, rl, cl, nd = load_currents.shape
    nt = block_library.shape[0]
    nb = rl * cl
    ng = n_r * rl // AGR * (cl // AGC)
    per_turn = GROUP * UNROLL
    slots = -(-(nb + nt * (GROUP - 1)) // per_turn) * per_turn
    vmem = pl.BlockSpec(memory_space=pltpu.VMEM)
    smem = pl.BlockSpec(memory_space=pltpu.SMEM)
    padded = pltpu.VMEM((rl + 2, cl + 2, sz, nd), F32)
    field = pltpu.VMEM((nb, sz, nd), F32)
    ordered = pltpu.VMEM((slots, sz, nd), F32)
    shape = jax.ShapeDtypeStruct((nb, sz, nd), F32)
    dma = pltpu.SemaphoreType.DMA
    order = pl.pallas_call(
        functools.partial(order_kernel, nt),
        out_shape=jax.ShapeDtypeStruct((8, 2 * nb), jnp.int32),
        in_specs=[vmem],
        out_specs=vmem,
    )(block_types)
    v, res = pl.pallas_call(
        functools.partial(kernel, n_r, n_c, rl, cl),
        out_shape=(shape, shape),
        in_specs=[pl.BlockSpec(memory_space=pl.ANY)] + [vmem] * 4 + [smem, smem],
        out_specs=(vmem, vmem),
        scratch_shapes=[
            padded, padded, field, field, field, ordered, ordered,
            pltpu.VMEM((nt, 2 * nd, 2 * nd), BF), pltpu.VMEM((nt, nd), F32), pltpu.VMEM((nt, nd), F32),
            pltpu.VMEM((2, nb), F32), pltpu.VMEM((n_r, 2, nb), F32),
            pltpu.VMEM((sz, nb), F32), pltpu.VMEM((n_r, sz, nb), F32),
            pltpu.VMEM((sz, nb), F32), pltpu.VMEM((n_r, sz, nb), F32),
            pltpu.VMEM((6, n_r, nb), F32), pltpu.VMEM((n_r // STEP, ng, STEP * nb), BF),
            pltpu.VMEM((ng, 2 * ng), F32), pltpu.VMEM((ng, nb), F32),
            pltpu.VMEM((3, ng, ng), BF), pltpu.VMEM((ng, 3 * ng), BF), pltpu.VMEM((ng, ng), F32),
            pltpu.VMEM((2, sz, ng), F32), pltpu.VMEM((2, sz, ng), F32), pltpu.VMEM((4, sz, nb), F32),
            pltpu.VMEM((6, sz, nd), F32), pltpu.VMEM((1, nd), F32), pltpu.VMEM((n_r, 1, nd), F32),
            pltpu.VMEM((1, nd), F32), pltpu.VMEM((n_c, 1, nd), F32),
            dma, dma, dma, dma, dma, dma,
            dma((2, 4)), dma((2, 4)), dma((2,)), dma((2,)),
            dma, dma, dma, dma, dma,
        ],
        compiler_params=pltpu.CompilerParams(
            collective_id=0, has_side_effects=True, vmem_limit_bytes=56 * 1024 * 1024
        ),
    )(
        load_currents.reshape(sz, nb, nd), block_library, strap_conductance,
        block_types, aggregate_map, block_types, order,
    )
    back = lambda x: jnp.swapaxes(x, 0, 1).reshape(load_currents.shape)
    return back(v), back(res)


def solution(mesh):
    placed = (P(None, "row", "col", None), P(), P(), P("row", "col"), P("row", "col"))
    return jax.shard_map(
        functools.partial(on_device, mesh.shape["row"], mesh.shape["col"]),
        mesh=mesh,
        in_specs=placed,
        out_specs=(P(None, "row", "col", None), P(None, "row", "col", None)),
        check_vma=False,
    )
```
